1024 devices in a mesh: row: 8 (over x, core), col: 128 (over y, z).
Axes of the slice: x: 4, y: 4, z: 32, core: 2. Of those that a mesh axis runs over, the one named last changes fastest.
Arguments:
- inputs: bfloat16 [512, 8192], P('col', 'row'), may hold values from -1.5 to 1.5
- grad_out: bfloat16 [512, 8192], P('col', 'row'), may hold values from -3 to 3
- gate: bfloat16 [512, 30720], P('row', 'col'), may hold values from -6 to 6
- up: bfloat16 [512, 30720], P('row', 'col'), may hold values from -6 to 6
- gate_weight: bfloat16 [8192, 30720], P('row', 'col'), may hold values from -0.0625 to 0.0625
- up_weight: bfloat16 [8192, 30720], P('row', 'col'), may hold values from -0.0625 to 0.0625
- down_weight: bfloat16 [30720, 8192], P('col', 'row'), may hold values from -0.03125 to 0.03125
Outputs:
- grad_inputs: bfloat16 [512, 8192], P('col', 'row')
- grad_gate_weight: bfloat16 [8192, 30720], P('row', 'col')
- grad_up_weight: bfloat16 [8192, 30720], P('row', 'col')
- grad_down_weight: bfloat16 [30720, 8192], P('col', 'row')
The draws below stay inside these ranges and needn't reach their ends.
All inputs are finite; a program needn't handle non-finite values.
Results may differ from the reference program's by a relative error of at most 0.022.
Values may be sent and summed in bfloat16 or wider, within the bound.
A program may use at most 32 MiB of HBM per device.

```python
import jax
import jax.numpy as jnp

D = 8192
FF = 30720
TOKENS = 512


def levels(stream_key, dims, split, smallest, high):
    def one(dim, parts):
        steps = jax.random.uniform(jax.random.fold_in(jax.random.fold_in(stream_key, 6), dim), (parts,), jnp.float32, smallest / len(split), high / len(split))
        return jnp.repeat(jnp.exp(steps), dims[dim] // parts).reshape((-1,) + (1,) * (len(dims) - dim - 1))

    level = one(*split[0])
    for cut in split[1:]:
        level = level * one(*cut)
    return level


def bell_draw(key, dims, width, reach, pieces=(), dtype=jnp.bfloat16):
    entries = width * jax.random.normal(key, dims, jnp.float32)
    if pieces:
        entries = entries * levels(key, dims, pieces, -0.22, 0.18)
    return jnp.clip(entries, -reach, reach).astype(dtype)


def setup_inputs(seed: int = 0) -> dict:
    key_list = jax.random.split(jax.random.key(seed), 8)
    inputs = bell_draw(key_list[0], (TOKENS, D), 0.25, 1.5, ((0, 128), (1, 8)))
    grad_out = bell_draw(key_list[1], (TOKENS, D), 0.5, 3.0, ((0, 128), (1, 8)))
    gate = bell_draw(key_list[2], (TOKENS, FF), 1.0, 6.0, ((0, 8), (1, 128)))
    up = bell_draw(key_list[3], (TOKENS, FF), 1.0, 6.0, ((0, 8), (1, 128)))
    gate_weight = bell_draw(key_list[4], (D, FF), D ** -0.5, 0.0625, ((0, 8), (1, 128)))
    up_weight = bell_draw(key_list[5], (D, FF), D ** -0.5, 0.0625, ((0, 8), (1, 128)))
    down_weight = bell_draw(key_list[6], (FF, D), FF ** -0.5, 0.03125, ((0, 128), (1, 8)))
    return dict(inputs=inputs, grad_out=grad_out, gate=gate, up=up, gate_weight=gate_weight, up_weight=up_weight, down_weight=down_weight)


def reference(inputs, grad_out, gate, up, gate_weight, up_weight, down_weight):
    gate_vals = gate.astype(jnp.float32)
    up_vals = up.astype(jnp.float32)
    grad_hidden = jnp.dot(grad_out, down_weight.T, preferred_element_type=jnp.float32)
    sigmoid_gate = jax.nn.sigmoid(gate_vals)
    activated = gate_vals * sigmoid_gate
    grad_gate = (grad_hidden * up_vals * sigmoid_gate * (1.0 + gate_vals * (1.0 - sigmoid_gate))).astype(jnp.bfloat16)
    grad_up = (grad_hidden * activated).astype(jnp.bfloat16)
    hidden = (activated * up_vals).astype(jnp.bfloat16)
    grad_inputs = (jnp.dot(grad_gate, gate_weight.T, preferred_element_type=jnp.float32)
                   + jnp.dot(grad_up, up_weight.T, preferred_element_type=jnp.float32)).astype(jnp.bfloat16)
    grad_gate_weight = jnp.dot(inputs.T, grad_gate, preferred_element_type=jnp.float32).astype(jnp.bfloat16)
    grad_up_weight = jnp.dot(inputs.T, grad_up, preferred_element_type=jnp.float32).astype(jnp.bfloat16)
    grad_down_weight = jnp.dot(hidden.T, grad_out, preferred_element_type=jnp.float32).astype(jnp.bfloat16)
    return grad_inputs, grad_gate_weight, grad_up_weight, grad_down_weight
```

```python
import jax
import jax.numpy as jnp
from jax import lax
from jax.experimental import pallas as pl
from jax.experimental.pallas import tpu as pltpu
from jax.sharding import PartitionSpec as P

MESH = pl.DeviceIdType.MESH
BF = jnp.bfloat16
F32 = jnp.float32

ROWS = 8
NY, NZ = 4, 32
NEAR, FAR = 4, 8
TOK = 4
TOKENS = 512
D = 1024
F = 240
H = D // 2
YB = 128
PB = 32
RB = 64


NT = (((1,), (1,)), ((), ()))
TN = (((0,), (0,)), ((), ()))


def al(x, n):
    return pl.multiple_of(x, n)


def kernel(
    in_hbm, out_hbm, gate_hbm, up_hbm, wg_hbm, wu_hbm, wd_hbm,
    gi_hbm, dwg_hbm, dwu_hbm, dwd_hbm,
    far_o, far_i, OUT, IN, wg, wu, wd, gate, up, fa, fb, hid,
    hp, hr, gh, gg, gu, s2, sp, sm, r2a, r2b, rm, rp, tb, sn, n1, n2, n3, n4,
    fs, fr, gi, dwg, dwu, dwd,
    ld_sem, st_sem,
    far_s, far_r, near_s, near_r, y_s, y_r, f_s, f_r,
    gu_s, gu_r, hp_s, hp_r, gh_s, gh_r,
    ry_s, ry_r, rn_s, rn_r, rf_s, rf_r,
):
    r = lax.axis_index("row")
    c = lax.axis_index("col")
    y = c // NZ
    z = c % NZ
    zl = z % NEAR
    zh = z // NEAR

    def at_z(dz):
        return (r, y * NZ + (z + dz + NZ) % NZ)

    def at_y(dy):
        return (r, ((y + dy + NY) % NY) * NZ + z)

    def at_row(dr):
        return ((r + dr) % ROWS, c)

    def remote(src, dst, ss, rs, dev):
        return pltpu.make_async_remote_copy(
            src_ref=src, dst_ref=dst, send_sem=ss, recv_sem=rs, device_id=dev, device_id_type=MESH
        )

    loads = [
        pltpu.make_async_copy(out_hbm, far_o.at[zh], ld_sem.at[0]),
        pltpu.make_async_copy(gate_hbm, gate.at[pl.ds(al(r * RB, RB), RB), :], ld_sem.at[1]),
        pltpu.make_async_copy(up_hbm, up.at[pl.ds(al(r * RB, RB), RB), :], ld_sem.at[2]),
        pltpu.make_async_copy(in_hbm, far_i.at[zh], ld_sem.at[3]),
        pltpu.make_async_copy(wd_hbm, wd, ld_sem.at[4]),
        pltpu.make_async_copy(wg_hbm, wg, ld_sem.at[5]),
        pltpu.make_async_copy(wu_hbm, wu, ld_sem.at[6]),
    ]
    for cp in loads:
        cp.start()

    barrier = pltpu.get_barrier_semaphore()
    partners = [at_z(NEAR * k) for k in range(1, FAR)] + [at_z(d) for d in (1, -1, 2, -2)]
    partners += [at_y(1), at_y(-1)] + [at_row(k) for k in range(1, ROWS)]
    for dev in partners:
        pl.semaphore_signal(barrier, inc=1, device_id=dev, device_id_type=MESH)
    pl.semaphore_wait(barrier, len(partners))

    pending = []

    def go(cp):
        cp.start()
        pending.append(cp)
        return cp

    def far_send(a, buf):
        return [
            go(remote(buf.at[zh], buf.at[zh], far_s.at[a, k], far_r.at[a, k], at_z(NEAR * k)))
            for k in range(1, FAR)
        ]

    def piece(yy, q):
        off = ((y + yy + NY) % NY) * YB + ((zl + q + NEAR) % NEAR) * PB
        return pl.ds(al(off, PB), PB)

    def far_done(a, cps, buf, full):
        for cp in cps:
            cp.wait_recv()
        for k in range(0, FAR, 4):
            block = jnp.concatenate([buf[k + j].astype(F32) for j in range(4)], axis=0)
            base = y * YB + zl * PB + k * TOK
            full[pl.ds(al(base, 4 * TOK), 4 * TOK), :] = block.astype(BF)

    LO, HI, ALL = pl.ds(0, H), pl.ds(H, H), pl.ds(0, D)

    def near_send(a, full):
        me = piece(0, 0)
        out = []
        for i, (dz, cols) in enumerate(((1, ALL), (-1, ALL), (2, LO), (-2, HI))):
            out.append(
                go(remote(full.at[me, cols], full.at[me, cols], near_s.at[a, i], near_r.at[a, i], at_z(dz)))
            )
        return out

    def y_send(a, full, q, i):
        rows = piece(0, q)
        return [
            go(remote(full.at[rows, :], full.at[rows, :], y_s.at[a, i, j], y_r.at[a, i, j], at_y(dy)))
            for j, dy in enumerate((1, -1))
        ]

    def y_forward(a, full, q, i, j):
        rows = piece(-1, q) if j == 0 else piece(1, q)
        cols = LO if j == 0 else HI
        return go(
            remote(full.at[rows, cols], full.at[rows, cols], f_s.at[a, i, j], f_r.at[a, i, j], at_y(1 if j == 0 else -1))
        )

    QS = (0, -1, 1, 2)

    loads[0].wait()
    far0 = far_send(0, far_o)

    loads[1].wait()
    loads[2].wait()
    mine = pl.ds(al(r * RB, RB), RB)
    gus = []
    for a, ref in enumerate((gate, up)):
        for k in range(1, ROWS):
            gus.append(go(remote(ref.at[mine, :], ref.at[mine, :], gu_s.at[a, k], gu_r.at[a, k], at_row(k))))

    far_done(0, far0, far_o, OUT)
    near0 = near_send(0, OUT)
    ys0 = [y_send(0, OUT, 0, 0)]
    near0[0].wait_recv()
    ys0.append(y_send(0, OUT, -1, 1))
    near0[1].wait_recv()
    ys0.append(y_send(0, OUT, 1, 2))
    near0[2].wait_recv()
    near0[3].wait_recv()
    ys0.append(y_send(0, OUT, 2, 3))

    loads[3].wait()
    far1 = far_send(1, far_i)

    for cp in gus:
        cp.wait_recv()
    ri = lax.broadcasted_iota(jnp.int32, (YB, YB), 0)
    ci = lax.broadcasted_iota(jnp.int32, (YB, YB), 1)
    want = ((ri // TOK) % FAR) * (NEAR * TOK) + (ri // PB) * TOK + ri % TOK
    perm = jnp.where(ci == want, 1.0, 0.0).astype(BF)
    for b in range(NY):
        rows = pl.ds(b * YB, YB)
        g = jnp.dot(perm, gate[rows, :], preferred_element_type=F32)
        u = jnp.dot(perm, up[rows, :], preferred_element_type=F32)
        s = 1.0 / (1.0 + jnp.exp(-g))
        act = g * s
        fa[rows, :] = u * s * (1.0 + g * (1.0 - s))
        fb[rows, :] = act
        hid[rows, :] = (act * u).astype(BF)

    loads[4].wait()
    hps = [None] * 8
    hp_of = {}

    def hidden_block(dy):
        yb = (y + dy + NY) % NY
        rows = pl.ds(al(yb * YB, YB), YB)
        part = lax.dot_general(OUT[rows, :], wd[...], NT, preferred_element_type=F32)
        hp[rows, :] = part.astype(BF)

    hidden_block(0)
    fw = []
    for i in range(4):
        ys0[i][0].wait_recv()
        fw.append(y_forward(0, OUT, QS[i], i, 0))
        ys0[i][1].wait_recv()
        fw.append(y_forward(0, OUT, QS[i], i, 1))
    hidden_block(-1)
    hidden_block(1)
    for cp in fw:
        cp.wait_recv()
    hidden_block(2)

    hpx = []
    for k in range(1, ROWS):
        dst_row = (r + k) % ROWS
        rows = pl.ds(al(dst_row * RB, RB), RB)
        hpx.append(go(remote(hp.at[rows, :], hr.at[k], hp_s.at[k], hp_r.at[k], at_row(k))))

    far_done(1, far1, far_i, IN)
    near1 = near_send(1, IN)
    ys1 = [y_send(1, IN, 0, 0)]

    acc = hp[mine, :].astype(F32)
    for k in range(1, ROWS):
        hpx[k - 1].wait_recv()
        acc = acc + hr[k].astype(F32)
    gh[mine, :] = acc.astype(BF)
    ghx = [go(remote(gh.at[mine, :], gh.at[mine, :], gh_s.at[k], gh_r.at[k], at_row(k))) for k in range(1, ROWS)]

    near1[0].wait_recv()
    ys1.append(y_send(1, IN, -1, 1))
    near1[1].wait_recv()
    ys1.append(y_send(1, IN, 1, 2))
    near1[2].wait_recv()
    near1[3].wait_recv()
    ys1.append(y_send(1, IN, 2, 3))

    for cp in ghx:
        cp.wait_recv()
    ghv = gh[...].astype(F32)
    gg[...] = (ghv * fa[...]).astype(BF)
    gu[...] = (ghv * fb[...]).astype(BF)
    loads[5].wait()
    loads[6].wait()

    def partial(dy):
        yb = (y + dy + NY) % NY
        rows = pl.ds(al(yb * YB, YB), YB)
        return lax.dot_general(gg[rows, :], wg[...], NT, preferred_element_type=F32) + lax.dot_general(
            gu[rows, :], wu[...], NT, preferred_element_type=F32
        )

    s2[...] = partial(2).astype(BF)
    ra = go(remote(s2.at[:, LO], r2a, ry_s.at[0], ry_r.at[0], at_y(1)))
    rb = go(remote(s2.at[:, HI], r2b, ry_s.at[1], ry_r.at[1], at_y(-1)))
    p1 = partial(1)
    m1 = partial(-1)
    tb[...] = partial(0)
    ra.wait_recv()
    sp[:, :H] = (p1[:, :H] + r2a[...].astype(F32)).astype(BF)
    sp[:, H:] = p1[:, H:].astype(BF)
    rpl = go(remote(sp, rm, ry_s.at[2], ry_r.at[2], at_y(1)))
    rb.wait_recv()
    sm[:, :H] = m1[:, :H].astype(BF)
    sm[:, H:] = (m1[:, H:] + r2b[...].astype(F32)).astype(BF)
    rmi = go(remote(sm, rp, ry_s.at[3], ry_r.at[3], at_y(-1)))

    dwd[...] = lax.dot_general(hid[...], OUT[...], TN, preferred_element_type=F32).astype(BF)
    st2 = pltpu.make_async_copy(dwd, dwd_hbm, st_sem.at[0])
    st2.start()

    rpl.wait_recv()
    rmi.wait_recv()
    tb[...] = tb[...] + rm[...].astype(F32) + rp[...].astype(F32)
    sn[...] = tb[...].astype(BF)

    def local_piece(q):
        return pl.ds(al(((zl + q + NEAR) % NEAR) * PB, PB), PB)

    nx = [
        go(remote(sn.at[local_piece(1), :], n1, rn_s.at[0], rn_r.at[0], at_z(1))),
        go(remote(sn.at[local_piece(-1), :], n2, rn_s.at[1], rn_r.at[1], at_z(-1))),
        go(remote(sn.at[local_piece(2), LO], n3, rn_s.at[2], rn_r.at[2], at_z(2))),
        go(remote(sn.at[local_piece(2), HI], n4, rn_s.at[3], rn_r.at[3], at_z(-2))),
    ]

    fw1 = []
    for i in range(4):
        ys1[i][0].wait_recv()
        fw1.append(y_forward(1, IN, QS[i], i, 0))
        ys1[i][1].wait_recv()
        fw1.append(y_forward(1, IN, QS[i], i, 1))

    for cp in nx:
        cp.wait_recv()
    own = tb[local_piece(0), :] + n1[...].astype(F32) + n2[...].astype(F32)
    lo = own[:, :H] + n3[...].astype(F32)
    hi = own[:, H:] + n4[...].astype(F32)
    for k in range(FAR):
        fs[k, :, :H] = lo[k * TOK:(k + 1) * TOK, :].astype(BF)
        fs[k, :, H:] = hi[k * TOK:(k + 1) * TOK, :].astype(BF)
    fx = []
    for k in range(1, FAR):
        dst = (zh + k) % FAR
        fx.append(go(remote(fs.at[dst], fr.at[k], rf_s.at[k], rf_r.at[k], at_z(NEAR * k))))

    for cp in fw1:
        cp.wait_recv()
    dwg[...] = lax.dot_general(IN[...], gg[...], TN, preferred_element_type=F32).astype(BF)
    st0 = pltpu.make_async_copy(dwg, dwg_hbm, st_sem.at[1])
    st0.start()
    dwu[...] = lax.dot_general(IN[...], gu[...], TN, preferred_element_type=F32).astype(BF)
    st1 = pltpu.make_async_copy(dwu, dwu_hbm, st_sem.at[2])
    st1.start()

    total = fs[zh].astype(F32)
    for k in range(1, FAR):
        fx[k - 1].wait_recv()
        total = total + fr[k].astype(F32)
    gi[...] = total.astype(BF)
    st3 = pltpu.make_async_copy(gi, gi_hbm, st_sem.at[3])
    st3.start()

    for cp in pending:
        cp.wait_send()
    for cp in (st0, st1, st2, st3):
        cp.wait()


def local(inputs, grad_out, gate, up, gate_weight, up_weight, down_weight):
    anyspec = pl.BlockSpec(memory_space=pl.ANY)
    V = pltpu.VMEM
    dma = pltpu.SemaphoreType.DMA
    scratch = [
        V((FAR, TOK, D), BF), V((FAR, TOK, D), BF),
        V((TOKENS, D), BF), V((TOKENS, D), BF),
        V((D, F), BF), V((D, F), BF), V((F, D), BF),
        V((TOKENS, F), BF), V((TOKENS, F), BF),
        V((TOKENS, F), F32), V((TOKENS, F), F32), V((TOKENS, F), BF),
        V((TOKENS, F), BF), V((ROWS, RB, F), BF), V((TOKENS, F), BF),
        V((TOKENS, F), BF), V((TOKENS, F), BF),
        V((YB, D), BF), V((YB, D), BF), V((YB, D), BF),
        V((YB, H), BF), V((YB, H), BF), V((YB, D), BF), V((YB, D), BF),
        V((YB, D), F32), V((YB, D), BF),
        V((PB, D), BF), V((PB, D), BF), V((PB, H), BF), V((PB, H), BF),
        V((FAR, TOK, D), BF), V((FAR, TOK, D), BF), V((TOK, D), BF),
        V((D, F), BF), V((D, F), BF), V((F, D), BF),
        dma((7,)), dma((4,)),
        dma((2, FAR)), dma((2, FAR)), dma((2, 4)), dma((2, 4)),
        dma((2, 4, 2)), dma((2, 4, 2)), dma((2, 4, 2)), dma((2, 4, 2)),
        dma((2, ROWS)), dma((2, ROWS)), dma((ROWS,)), dma((ROWS,)), dma((ROWS,)), dma((ROWS,)),
        dma((4,)), dma((4,)), dma((4,)), dma((4,)), dma((FAR,)), dma((FAR,)),
    ]
    return pl.pallas_call(
        kernel,
        out_shape=(
            jax.ShapeDtypeStruct((TOK, D), BF),
            jax.ShapeDtypeStruct((D, F), BF),
            jax.ShapeDtypeStruct((D, F), BF),
            jax.ShapeDtypeStruct((F, D), BF),
        ),
        in_specs=[anyspec] * 7,
        out_specs=[anyspec] * 4,
        scratch_shapes=scratch,
        compiler_params=pltpu.CompilerParams(
            collective_id=0, has_side_effects=True, vmem_limit_bytes=48 * 1024 * 1024
        ),
    )(inputs, grad_out, gate, up, gate_weight, up_weight, down_weight)


def solution(mesh):
    return jax.shard_map(
        local,
        mesh=mesh,
        in_specs=(
            P("col", "row"), P("col", "row"), P("row", "col"), P("row", "col"),
            P("row", "col"), P("row", "col"), P("col", "row"),
        ),
        out_specs=(P("col", "row"), P("row", "col"), P("row", "col"), P("col", "row")),
        check_vma=False,
    )
```

```python
import jax
import jax.numpy as jnp
from jax import lax
from jax.experimental import pallas as pl
from jax.experimental.pallas import tpu as pltpu
from jax.sharding import PartitionSpec as P

MESH = pl.DeviceIdType.MESH
BF = jnp.bfloat16
F32 = jnp.float32

ROWS = 8
NY, NZ = 4, 32
NEAR, FAR = 4, 8
TOK = 4
TOKENS = 512
D = 1024
F = 240
H = D // 2
YB = 128
PB = 32
RB = 64
EB = YB // 8


NT = (((1,), (1,)), ((), ()))
TN = (((0,), (0,)), ((), ()))


def al(x, n):
    return pl.multiple_of(x, n)


def kernel(
    in_hbm, out_hbm, gate_hbm, up_hbm, wg_hbm, wu_hbm, wd_hbm,
    gi, dwg, dwu, dwd,
    far_o, far_i, OUT, IN, wg, wu, wd, gate, up, fa, fb, hid,
    hp0, hpa, hpb, hr0, hra, hrb, gh0, gha, ghb, gg, gu, s2, sp, sm, r2, rm, rp, tb, sn, n1, n2, n3, n4,
    fs, ff, c1p, c1m, c2p, c2m, c3p, c3m, c4l, c4h, e2p, e2m,
    ld_sem,
    far_s, far_r, fw_s, fw_r, near_s, near_r, y_s, y_r, f_s, f_r,
    gu_s, gu_r, hp_s, hp_r, gh_s, gh_r,
    ry_s, ry_r, rn_s, rn_r, rf_s, rf_r,
):
    r = lax.axis_index("row")
    c = lax.axis_index("col")
    y = c // NZ
    z = c % NZ
    zl = z % NEAR
    zh = z // NEAR

    def at_z(dz):
        return (r, y * NZ + (z + dz + NZ) % NZ)

    def at_y(dy):
        return (r, ((y + dy + NY) % NY) * NZ + z)

    def at_row(dr):
        return ((r + dr) % ROWS, c)

    def remote(src, dst, ss, rs, dev):
        return pltpu.make_async_remote_copy(
            src_ref=src, dst_ref=dst, send_sem=ss, recv_sem=rs, device_id=dev, device_id_type=MESH
        )

    barrier = pltpu.get_barrier_semaphore()
    partners = [at_z(d) for d in (8, -8, 4, -4, 2, -2, 1, -1)] + [at_y(d) for d in (2, 1, -1)]
    partners += [at_row(k) for k in range(1, ROWS)]
    for dev in partners:
        pl.semaphore_signal(barrier, inc=1, device_id=dev, device_id_type=MESH)

    loads = [
        pltpu.make_async_copy(out_hbm, far_o.at[zh], ld_sem.at[0]),
        pltpu.make_async_copy(gate_hbm, gate.at[pl.ds(al(r * RB, RB), RB), :], ld_sem.at[1]),
        pltpu.make_async_copy(up_hbm, up.at[pl.ds(al(r * RB, RB), RB), :], ld_sem.at[2]),
        pltpu.make_async_copy(in_hbm, far_i.at[zh], ld_sem.at[3]),
        pltpu.make_async_copy(wd_hbm, wd, ld_sem.at[4]),
        pltpu.make_async_copy(wg_hbm, wg, ld_sem.at[5]),
        pltpu.make_async_copy(wu_hbm, wu, ld_sem.at[6]),
    ]
    for cp in loads:
        cp.start()
    loads[0].wait()
    pl.semaphore_wait(barrier, len(partners))

    pending = []

    def go(cp):
        cp.start()
        pending.append(cp)
        return cp

    LO, HI, ALL = pl.ds(0, H), pl.ds(H, H), pl.ds(0, D)

    def far_direct(a, buf):
        return [
            go(remote(buf.at[zh], buf.at[zh], far_s.at[a, j], far_r.at[a, j], at_z(NEAR * d)))
            for j, d in enumerate((2, -2, 1, -1))
        ]

    def far_forward(a, buf, direct):
        out = []
        for j, (d, cols) in enumerate(((1, LO), (-1, HI))):
            direct[j].wait_recv()
            slot = (zh - 2 * d + FAR) % FAR
            out.append(go(remote(buf.at[slot], buf.at[slot], fw_s.at[a, j, 0], fw_r.at[a, j, 0], at_z(NEAR * d))))
            out.append(
                go(
                    remote(
                        buf.at[slot, :, cols], buf.at[slot, :, cols],
                        fw_s.at[a, j, 1], fw_r.at[a, j, 1], at_z(2 * NEAR * d),
                    )
                )
            )
        return out

    def piece(yy, q):
        off = ((y + yy + NY) % NY) * YB + ((zl + q + NEAR) % NEAR) * PB
        return pl.ds(al(off, PB), PB)

    def far_done(cps, buf, full):
        for cp in cps:
            cp.wait_recv()
        for k in range(0, FAR, 4):
            block = jnp.concatenate([buf[k + j].astype(F32) for j in range(4)], axis=0)
            base = y * YB + zl * PB + k * TOK
            full[pl.ds(al(base, 4 * TOK), 4 * TOK), :] = block.astype(BF)

    def near_send(a, full):
        me = piece(0, 0)
        return [
            go(remote(full.at[me, cols], full.at[me, cols], near_s.at[a, i], near_r.at[a, i], at_z(dz)))
            for i, (dz, cols) in enumerate(((1, ALL), (-1, ALL), (2, LO), (-2, HI)))
        ]

    def y_send(a, full, q, i):
        rows = piece(0, q)
        return [
            go(remote(full.at[rows, :], full.at[rows, :], y_s.at[a, i, j], y_r.at[a, i, j], at_y(dy)))
            for j, dy in enumerate((1, -1))
        ]

    def y_forward(a, full, q, i, j):
        rows = piece(-1, q) if j == 0 else piece(1, q)
        cols = LO if j == 0 else HI
        return go(
            remote(full.at[rows, cols], full.at[rows, cols], f_s.at[a, i, j], f_r.at[a, i, j], at_y(1 if j == 0 else -1))
        )

    def near_to_y(a, full, near, ys):
        near[0].wait_recv()
        ys.append(y_send(a, full, -1, 1))
        near[1].wait_recv()
        ys.append(y_send(a, full, 1, 2))
        near[2].wait_recv()
        near[3].wait_recv()
        ys.append(y_send(a, full, 2, 3))

    def forwards(a, full, ys):
        fw = []
        for i in range(4):
            for j in range(2):
                ys[i][j].wait_recv()
                fw.append(y_forward(a, full, QS[i], i, j))
        return fw

    QS = (0, -1, 1, 2)

    far0 = far_direct(0, far_o)

    loads[1].wait()
    loads[2].wait()
    mine = pl.ds(al(r * RB, RB), RB)
    gus = []
    for a, ref in enumerate((gate, up)):
        for k in range(1, ROWS):
            gus.append(go(remote(ref.at[mine, :], ref.at[mine, :], gu_s.at[a, k], gu_r.at[a, k], at_row(k))))

    ffw0 = far_forward(0, far_o, far0)
    far_done(far0[2:] + ffw0, far_o, OUT)
    near0 = near_send(0, OUT)
    ys0 = [y_send(0, OUT, 0, 0)]
    near_to_y(0, OUT, near0, ys0)
    loads[3].wait()
    far1 = far_direct(1, far_i)

    for cp in gus:
        cp.wait_recv()
    ri = lax.broadcasted_iota(jnp.int32, (YB, YB), 0)
    ci = lax.broadcasted_iota(jnp.int32, (YB, YB), 1)
    want = ((ri // TOK) % FAR) * (NEAR * TOK) + (ri // PB) * TOK + ri % TOK
    perm = jnp.where(ci == want, 1.0, 0.0).astype(BF)
    for b in range(NY):
        rows = pl.ds(b * YB, YB)
        g = jnp.dot(perm, gate[rows, :], preferred_element_type=F32)
        u = jnp.dot(perm, up[rows, :], preferred_element_type=F32)
        s = 1.0 / (1.0 + jnp.exp(-g))
        act = g * s
        fa[rows, :] = u * s * (1.0 + g * (1.0 - s))
        fb[rows, :] = act
        hid[rows, :] = (act * u).astype(BF)

    loads[4].wait()

    def y_rows(dy):
        return pl.ds(al(((y + dy + NY) % NY) * YB, YB), YB)

    def hidden_block(dy, dst, i):
        part = lax.dot_general(OUT[y_rows(dy), :], wd[...], NT, preferred_element_type=F32)
        dst[:, i * EB:(i + 1) * EB, :] = part.astype(BF).reshape(ROWS, EB, F)

    def row_out(src, dst, b):
        cps = []
        for k in range(1, ROWS):
            cps.append(go(remote(src.at[(r + k) % ROWS], dst.at[k], hp_s.at[b, k], hp_r.at[b, k], at_row(k))))
        return cps

    def row_back(cps, own, got, dst, b):
        acc = own[r].astype(F32)
        for k in range(1, ROWS):
            cps[k - 1].wait_recv()
            acc = acc + got[k].astype(F32)
        dst[r] = acc.astype(BF)
        return [go(remote(dst.at[r], dst.at[r], gh_s.at[b, k], gh_r.at[b, k], at_row(k))) for k in range(1, ROWS)]

    def gated(dy, src, i):
        rows = y_rows(dy)
        v = src[:, i * EB:(i + 1) * EB, :].reshape(YB, F).astype(F32)
        gg[rows, :] = (v * fa[rows, :]).astype(BF)
        gu[rows, :] = (v * fb[rows, :]).astype(BF)

    def partial(dy):
        rows = y_rows(dy)
        return jnp.dot(gg[rows, :], wg[...], preferred_element_type=F32) + jnp.dot(
            gu[rows, :], wu[...], preferred_element_type=F32
        )

    hidden_block(0, hp0, 0)
    x0 = row_out(hp0, hr0, 0)
    fw0 = forwards(0, OUT, ys0)
    hidden_block(-1, hpa, 0)
    hidden_block(1, hpa, 1)
    xa = row_out(hpa, hra, 1)
    g0 = row_back(x0, hp0, hr0, gh0, 0)
    ffw1 = far_forward(1, far_i, far1)
    for cp in fw0:
        cp.wait_recv()
    hidden_block(2, hpb, 0)
    xb = row_out(hpb, hrb, 2)
    ga = row_back(xa, hpa, hra, gha, 1)
    gb = row_back(xb, hpb, hrb, ghb, 2)
    far_done(far1[2:] + ffw1, far_i, IN)
    near1 = near_send(1, IN)

    loads[5].wait()
    loads[6].wait()
    for cp in ga:
        cp.wait_recv()
    gated(1, gha, 1)
    sp[...] = partial(1).astype(BF)
    go_p = go(remote(sp, rm, ry_s.at[0], ry_r.at[0], at_y(1)))
    gated(-1, gha, 0)
    sm[...] = partial(-1).astype(BF)
    go_m = go(remote(sm, rp, ry_s.at[1], ry_r.at[1], at_y(-1)))
    for cp in g0:
        cp.wait_recv()
    gated(0, gh0, 0)
    tb[...] = partial(0)
    for cp in gb:
        cp.wait_recv()
    gated(2, ghb, 0)

    def local_piece(q):
        return pl.ds(al(((zl + q + NEAR) % NEAR) * PB, PB), PB)

    RQ = (2, 1, -1, 0)
    s2[...] = partial(2).astype(BF)
    far_y = [
        go(remote(s2.at[local_piece(q), :], r2.at[local_piece(q), :], ry_s.at[2 + i], ry_r.at[2 + i], at_y(2)))
        for i, q in enumerate(RQ)
    ]
    ys1 = [y_send(1, IN, 0, 0)]
    near_to_y(1, IN, near1, ys1)
    dwd[...] = lax.dot_general(hid[...], OUT[...], TN, preferred_element_type=F32).astype(BF)

    go_p.wait_recv()
    go_m.wait_recv()
    tb[...] = tb[...] + rm[...].astype(F32) + rp[...].astype(F32)
    nx = []
    for i, q in enumerate(RQ):
        rows = local_piece(q)
        far_y[i].wait_recv()
        v = tb[rows, :] + r2[rows, :].astype(F32)
        if q == 0:
            tb[rows, :] = v
            continue
        sn[rows, :] = v.astype(BF)
        if q == 2:
            nx.append(go(remote(sn.at[rows, LO], n3, rn_s.at[2], rn_r.at[2], at_z(2))))
            nx.append(go(remote(sn.at[rows, HI], n4, rn_s.at[3], rn_r.at[3], at_z(-2))))
        elif q == 1:
            nx.append(go(remote(sn.at[rows, :], n1, rn_s.at[0], rn_r.at[0], at_z(1))))
        else:
            nx.append(go(remote(sn.at[rows, :], n2, rn_s.at[1], rn_r.at[1], at_z(-1))))

    for cp in nx:
        cp.wait_recv()
    own = tb[local_piece(0), :] + n1[...].astype(F32) + n2[...].astype(F32)
    lo = own[:, :H] + n3[...].astype(F32)
    hi = own[:, H:] + n4[...].astype(F32)
    for k in range(FAR):
        ff[k, :, :H] = lo[k * TOK:(k + 1) * TOK, :]
        ff[k, :, H:] = hi[k * TOK:(k + 1) * TOK, :]
    for k in range(FAR):
        fs[k] = ff[k].astype(BF)

    def dest(d):
        return (zh + d + FAR) % FAR

    x4l = go(remote(fs.at[dest(4), :, LO], c4l, rf_s.at[0], rf_r.at[0], at_z(2 * NEAR)))
    x4h = go(remote(fs.at[dest(4), :, HI], c4h, rf_s.at[1], rf_r.at[1], at_z(-2 * NEAR)))
    x3p = go(remote(fs.at[dest(3)], c3p, rf_s.at[2], rf_r.at[2], at_z(NEAR)))
    x3m = go(remote(fs.at[dest(-3)], c3m, rf_s.at[3], rf_r.at[3], at_z(-NEAR)))
    x1p = go(remote(fs.at[dest(1)], c1p, rf_s.at[4], rf_r.at[4], at_z(NEAR)))
    x1m = go(remote(fs.at[dest(-1)], c1m, rf_s.at[5], rf_r.at[5], at_z(-NEAR)))
    fw1 = forwards(1, IN, ys1)
    x3p.wait_recv()
    x4l.wait_recv()
    v = ff[dest(2)] + c3p[...].astype(F32)
    e2p[:, :H] = (v[:, :H] + c4l[...].astype(F32)).astype(BF)
    e2p[:, H:] = v[:, H:].astype(BF)
    x2p = go(remote(e2p, c2p, rf_s.at[6], rf_r.at[6], at_z(2 * NEAR)))
    x3m.wait_recv()
    x4h.wait_recv()
    v = ff[dest(-2)] + c3m[...].astype(F32)
    e2m[:, :H] = v[:, :H].astype(BF)
    e2m[:, H:] = (v[:, H:] + c4h[...].astype(F32)).astype(BF)
    x2m = go(remote(e2m, c2m, rf_s.at[7], rf_r.at[7], at_z(-2 * NEAR)))
    for cp in fw1:
        cp.wait_recv()
    dwg[...] = lax.dot_general(gg[...], IN[...], TN, preferred_element_type=F32).astype(BF)
    dwu[...] = lax.dot_general(gu[...], IN[...], TN, preferred_element_type=F32).astype(BF)
    total = ff[zh]
    for cp, ref in ((x1p, c1p), (x1m, c1m), (x2p, c2p), (x2m, c2m)):
        cp.wait_recv()
        total = total + ref[...].astype(F32)
    gi[...] = total.astype(BF)

    for cp in pending:
        cp.wait_send()


def store(*refs):
    for src, dst in zip(refs[:4], refs[4:]):
        dst[...] = src[...]


def local(inputs, grad_out, gate, up, gate_weight, up_weight, down_weight):
    anyspec = pl.BlockSpec(memory_space=pl.ANY)
    V = pltpu.VMEM
    dma = pltpu.SemaphoreType.DMA
    four = V((TOK, D), BF)
    scratch = [
        V((FAR, TOK, D), BF), V((FAR, TOK, D), BF),
        V((TOKENS, D), BF), V((TOKENS, D), BF),
        V((F, D), BF), V((F, D), BF), V((F, D), BF),
        V((TOKENS, F), BF), V((TOKENS, F), BF),
        V((TOKENS, F), F32), V((TOKENS, F), F32), V((TOKENS, F), BF),
        V((ROWS, EB, F), BF), V((ROWS, 2 * EB, F), BF), V((ROWS, EB, F), BF),
        V((ROWS, EB, F), BF), V((ROWS, 2 * EB, F), BF), V((ROWS, EB, F), BF),
        V((ROWS, EB, F), BF), V((ROWS, 2 * EB, F), BF), V((ROWS, EB, F), BF),
        V((TOKENS, F), BF), V((TOKENS, F), BF),
        V((YB, D), BF), V((YB, D), BF), V((YB, D), BF),
        V((YB, D), BF), V((YB, D), BF), V((YB, D), BF),
        V((YB, D), F32), V((YB, D), BF),
        V((PB, D), BF), V((PB, D), BF), V((PB, H), BF), V((PB, H), BF),
        V((FAR, TOK, D), BF), V((FAR, TOK, D), F32),
        four, four, four, four, four, four, V((TOK, H), BF), V((TOK, H), BF), four, four,
        dma((7,)),
        dma((2, 4)), dma((2, 4)), dma((2, 2, 2)), dma((2, 2, 2)), dma((2, 4)), dma((2, 4)),
        dma((2, 4, 2)), dma((2, 4, 2)), dma((2, 4, 2)), dma((2, 4, 2)),
        dma((2, ROWS)), dma((2, ROWS)), dma((3, ROWS)), dma((3, ROWS)), dma((3, ROWS)), dma((3, ROWS)),
        dma((6,)), dma((6,)), dma((4,)), dma((4,)), dma((8,)), dma((8,)),
    ]
    shapes = (
        jax.ShapeDtypeStruct((TOK, D), BF),
        jax.ShapeDtypeStruct((F, D), BF),
        jax.ShapeDtypeStruct((F, D), BF),
        jax.ShapeDtypeStruct((F, D), BF),
    )
    vm = pl.BlockSpec(memory_space=pltpu.VMEM)
    args = (inputs, grad_out, gate, up, gate_weight.T, up_weight.T, down_weight)
    made = pl.pallas_call(
        kernel,
        out_shape=shapes,
        in_specs=[anyspec] * 7,
        out_specs=[vm] * 4,
        scratch_shapes=scratch,
        compiler_params=pltpu.CompilerParams(
            collective_id=0, has_side_effects=True, vmem_limit_bytes=40 * 1024 * 1024
        ),
    )(*[pltpu.with_memory_space_constraint(x, pltpu.HBM) for x in args])
    gi, dwg, dwu, dwd = pl.pallas_call(
        store,
        out_shape=shapes,
        in_specs=[vm] * 4,
        out_specs=[vm] * 4,
    )(*[pltpu.with_memory_space_constraint(x, pltpu.VMEM) for x in made])
    return gi, dwg.T, dwu.T, dwd


def solution(mesh):
    return jax.shard_map(
        local,
        mesh=mesh,
        in_specs=(
            P("col", "row"), P("col", "row"), P("row", "col"), P("row", "col"),
            P("row", "col"), P("row", "col"), P("col", "row"),
        ),
        out_specs=(P("col", "row"), P("row", "col"), P("row", "col"), P("col", "row")),
        check_vma=False,
    )
```

```python
import jax
import jax.numpy as jnp
from jax import lax
from jax.experimental import pallas as pl
from jax.experimental.pallas import tpu as pltpu
from jax.sharding import PartitionSpec as P

MESH = pl.DeviceIdType.MESH
BF = jnp.bfloat16
F32 = jnp.float32

ROWS = 8
NY, NZ = 4, 32
NEAR, FAR = 4, 8
TOK = 4
TOKENS = 512
D = 1024
F = 240
H = D // 2
YB = 128
PB = 32
RB = 64
EB = YB // 8


NT = (((1,), (1,)), ((), ()))
TN = (((0,), (0,)), ((), ()))


def al(x, n):
    return pl.multiple_of(x, n)


def kernel(
    in_hbm, out_hbm, gate_hbm, up_hbm, wg_hbm, wu_hbm, wd_hbm,
    gi, dwg, dwu, dwd,
    o4, i4, OUT, IN, wg, wu, wd, gate, up, fa, fb, hid,
    hp0, hpa, hpb, hr0, hra, hrb, gh0, gha, ghb, gg, gu, s2, sp, sm, r2, rm, rp, tb, sn, n1, n2, n3, n4,
    fs, ff, c1p, c1m, c2p, c2m, c3p, c3m, c4l, c4h, e2p, e2m,
    ld_sem,
    far_s, far_r, fw_s, fw_r, q_s, q_r, near_s, near_r, y_s, y_r, f_s, f_r,
    gu_s, gu_r, hp_s, hp_r, gh_s, gh_r,
    ry_s, ry_r, rn_s, rn_r, rf_s, rf_r,
):
    r = lax.axis_index("row")
    c = lax.axis_index("col")
    y = c // NZ
    z = c % NZ

    def at_z(dz):
        return (r, y * NZ + (z + dz + NZ) % NZ)

    def at_y(dy, dz=0):
        return (r, ((y + dy + NY) % NY) * NZ + (z + dz + NZ) % NZ)

    def at_row(dr):
        return ((r + dr) % ROWS, c)

    def remote(src, dst, ss, rs, dev):
        return pltpu.make_async_remote_copy(
            src_ref=src, dst_ref=dst, send_sem=ss, recv_sem=rs, device_id=dev, device_id_type=MESH
        )

    barrier = pltpu.get_barrier_semaphore()
    partners = [at_z(d) for d in (8, -8, 4, -4, 2, -2, 1, -1)] + [at_y(d) for d in (2, 1, -1)]
    partners += [at_y(dy, dz) for dy in (2, 1, -1) for dz in (2, -2, 1, -1)]
    partners += [at_row(k) for k in range(1, ROWS)]
    for dev in partners:
        pl.semaphore_signal(barrier, inc=1, device_id=dev, device_id_type=MESH)

    loads = [
        pltpu.make_async_copy(out_hbm, o4.at[0, 0, 2], ld_sem.at[0]),
        pltpu.make_async_copy(gate_hbm, gate.at[pl.ds(al(r * RB, RB), RB), :], ld_sem.at[1]),
        pltpu.make_async_copy(up_hbm, up.at[pl.ds(al(r * RB, RB), RB), :], ld_sem.at[2]),
        pltpu.make_async_copy(in_hbm, i4.at[0, 0, 2], ld_sem.at[3]),
        pltpu.make_async_copy(wd_hbm, wd, ld_sem.at[4]),
        pltpu.make_async_copy(wg_hbm, wg, ld_sem.at[5]),
        pltpu.make_async_copy(wu_hbm, wu, ld_sem.at[6]),
    ]
    for cp in loads:
        cp.start()
    loads[0].wait()
    pl.semaphore_wait(barrier, len(partners))

    pending = []

    def go(cp):
        cp.start()
        pending.append(cp)
        return cp

    LO, HI = pl.ds(0, H), pl.ds(H, H)

    DY = (0, -1, 1, 2)
    FIRST, LAST, SHIFTED, ALLF = pl.ds(0, 5), pl.ds(5, 3), pl.ds(4, 3), pl.ds(0, FAR)

    def far_direct(a, buf):
        return [
            go(remote(buf.at[0, 0, 2], buf.at[0, 0, slot], far_s.at[a, j], far_r.at[a, j], at_z(NEAR * d)))
            for j, (d, slot) in enumerate(((2, 0), (-2, 4), (1, 1), (-1, 3)))
        ]

    def far_forward(a, buf, direct):
        out = []
        for j, (d, src, dst, cols) in enumerate(((1, 0, 7, LO), (-1, 4, 5, HI))):
            direct[j].wait_recv()
            out.append(
                go(remote(buf.at[0, 0, src], buf.at[0, 0, dst], fw_s.at[a, j, 0], fw_r.at[a, j, 0], at_z(NEAR * d)))
            )
            out.append(
                go(
                    remote(
                        buf.at[0, 0, src, :, cols], buf.at[0, 0, 6, :, cols],
                        fw_s.at[a, j, 1], fw_r.at[a, j, 1], at_z(2 * NEAR * d),
                    )
                )
            )
        return out

    def near_send(a, buf, part):
        return [
            go(remote(buf.at[0, 0, part], buf.at[0, p, part], near_s.at[a, p], near_r.at[a, p], at_z(dz)))
            for p, dz in ((1, 1), (2, -1), (3, 2))
        ]

    def y_send(a, buf, part, p):
        return [
            go(remote(buf.at[0, p, part], buf.at[b, p, part], y_s.at[a, p, j], y_r.at[a, p, j], at_y(dy)))
            for j, (b, dy) in enumerate(((1, 1), (2, -1)))
        ]

    def y_forward(a, buf, part, ys):
        out = []
        for p in range(NEAR):
            for j, (b, dy, cols) in enumerate(((1, 1, LO), (2, -1, HI))):
                ys[p][j].wait_recv()
                out.append(
                    go(
                        remote(
                            buf.at[b, p, part, :, cols], buf.at[3, p, part, :, cols],
                            f_s.at[a, p, j], f_r.at[a, p, j], at_y(dy),
                        )
                    )
                )
        return out

    def near_to_y(a, buf, part, near):
        ys = [y_send(a, buf, part, 0)]
        for p in (1, 2, 3):
            near[p - 1].wait_recv()
            ys.append(y_send(a, buf, part, p))
        return ys

    def merge(buf, full, b, half):
        for p in range(NEAR):
            block = jnp.concatenate([buf[b, p, 4 * half + j].astype(F32) for j in range(4)], axis=0)
            at = b * YB + p * PB + half * 4 * TOK
            full[at:at + 4 * TOK, :] = block.astype(BF)

    far0 = far_direct(0, o4)

    loads[1].wait()
    loads[2].wait()
    mine = pl.ds(al(r * RB, RB), RB)
    gus = []
    for a, ref in enumerate((gate, up)):
        for k in range(1, ROWS):
            gus.append(go(remote(ref.at[mine, :], ref.at[mine, :], gu_s.at[a, k], gu_r.at[a, k], at_row(k))))

    ffw0 = far_forward(0, o4, far0)
    far0[2].wait_recv()
    far0[3].wait_recv()
    near0 = near_send(0, o4, FIRST)
    ys0 = near_to_y(0, o4, FIRST, near0)
    merge(o4, OUT, 0, 0)
    for cp in ffw0:
        cp.wait_recv()
    rest = [[None] * NEAR for _ in range(NY)]
    for b, dy in ((3, 2), (1, 1), (2, -1), (0, 0)):
        for p, dz, part in ((3, -2, SHIFTED), (1, 1, LAST), (2, -1, LAST), (0, 0, LAST)):
            if b or p:
                rest[b][p] = go(
                    remote(o4.at[0, 0, part], o4.at[b, p, LAST], q_s.at[b, p], q_r.at[b, p], at_y(dy, dz))
                )
    fw0 = y_forward(0, o4, FIRST, ys0)
    merge(o4, OUT, 1, 0)
    merge(o4, OUT, 2, 0)

    for cp in gus:
        cp.wait_recv()
    ri = lax.broadcasted_iota(jnp.int32, (YB, YB), 0)
    ci = lax.broadcasted_iota(jnp.int32, (YB, YB), 1)
    near_i = ri // PB
    step = jnp.where(near_i == 0, 0, jnp.where(near_i == 1, -1, jnp.where(near_i == 2, 1, -2)))
    want = ((z + step + NEAR * ((ri // TOK) % FAR - 2) + 2 * NZ) % NZ) * TOK + ri % TOK
    perm = jnp.where(ci == want, 1.0, 0.0).astype(BF)
    for b in range(NY):
        src = pl.ds(al(((y + DY[b] + NY) % NY) * YB, YB), YB)
        rows = pl.ds(b * YB, YB)
        g = jnp.dot(perm, gate[src, :], preferred_element_type=F32)
        u = jnp.dot(perm, up[src, :], preferred_element_type=F32)
        s = 1.0 / (1.0 + jnp.exp(-g))
        act = g * s
        fa[rows, :] = u * s * (1.0 + g * (1.0 - s))
        fb[rows, :] = act
        hid[rows, :] = (act * u).astype(BF)

    loads[4].wait()

    def y_rows(b):
        return pl.ds(b * YB, YB)

    def arrived(b):
        for cp in rest[b]:
            if cp is not None:
                cp.wait_recv()
        merge(o4, OUT, b, 1)

    def hidden_block(b, dst, i):
        part = lax.dot_general(OUT[y_rows(b), :], wd[...], NT, preferred_element_type=F32)
        dst[:, i * EB:(i + 1) * EB, :] = part.astype(BF).reshape(ROWS, EB, F)

    def row_out(src, dst, b):
        cps = []
        for k in range(1, ROWS):
            cps.append(go(remote(src.at[(r + k) % ROWS], dst.at[k], hp_s.at[b, k], hp_r.at[b, k], at_row(k))))
        return cps

    def row_back(cps, own, got, dst, b):
        acc = own[r].astype(F32)
        for k in range(1, ROWS):
            cps[k - 1].wait_recv()
            acc = acc + got[k].astype(F32)
        dst[r] = acc.astype(BF)
        return [go(remote(dst.at[r], dst.at[r], gh_s.at[b, k], gh_r.at[b, k], at_row(k))) for k in range(1, ROWS)]

    def gated(b, src, i):
        rows = y_rows(b)
        v = src[:, i * EB:(i + 1) * EB, :].reshape(YB, F).astype(F32)
        gg[rows, :] = (v * fa[rows, :]).astype(BF)
        gu[rows, :] = (v * fb[rows, :]).astype(BF)

    def partial(b):
        rows = y_rows(b)
        return jnp.dot(gg[rows, :], wg[...], preferred_element_type=F32) + jnp.dot(
            gu[rows, :], wu[...], preferred_element_type=F32
        )

    arrived(0)
    hidden_block(0, hp0, 0)
    x0 = row_out(hp0, hr0, 0)
    arrived(1)
    hidden_block(1, hpa, 0)
    arrived(2)
    hidden_block(2, hpa, 1)
    xa = row_out(hpa, hra, 1)
    loads[3].wait()
    far1 = far_direct(1, i4)
    for cp in fw0:
        cp.wait_recv()
    merge(o4, OUT, 3, 0)
    arrived(3)
    hidden_block(3, hpb, 0)
    xb = row_out(hpb, hrb, 2)
    g0 = row_back(x0, hp0, hr0, gh0, 0)
    ga = row_back(xa, hpa, hra, gha, 1)
    gb = row_back(xb, hpb, hrb, ghb, 2)
    ffw1 = far_forward(1, i4, far1)

    loads[5].wait()
    loads[6].wait()
    for cp in ga:
        cp.wait_recv()
    gated(2, gha, 1)
    sp[...] = partial(2).astype(BF)
    go_p = go(remote(sp, rm, ry_s.at[0], ry_r.at[0], at_y(1)))
    gated(1, gha, 0)
    sm[...] = partial(1).astype(BF)
    go_m = go(remote(sm, rp, ry_s.at[1], ry_r.at[1], at_y(-1)))
    for cp in g0:
        cp.wait_recv()
    gated(0, gh0, 0)
    tb[...] = partial(0)
    for cp in gb:
        cp.wait_recv()
    gated(3, ghb, 0)

    def local_piece(p):
        return pl.ds(p * PB, PB)

    RQ = (3, 2, 1, 0)
    s2[...] = partial(3).astype(BF)
    far_y = [
        go(remote(s2.at[local_piece(q), :], r2.at[local_piece(q), :], ry_s.at[2 + i], ry_r.at[2 + i], at_y(2)))
        for i, q in enumerate(RQ)
    ]
    for cp in far1[2:] + ffw1:
        cp.wait_recv()
    near1 = near_send(1, i4, ALLF)
    dwd[...] = lax.dot_general(hid[...], OUT[...], TN, preferred_element_type=F32).astype(BF)

    go_p.wait_recv()
    go_m.wait_recv()
    tb[...] = tb[...] + rm[...].astype(F32) + rp[...].astype(F32)
    nx = []
    for i, q in enumerate(RQ):
        rows = local_piece(q)
        far_y[i].wait_recv()
        v = tb[rows, :] + r2[rows, :].astype(F32)
        if q == 0:
            tb[rows, :] = v
            continue
        if q == 3:
            sn[rows, :H] = jnp.concatenate([v[TOK:, :H], v[:TOK, :H]], axis=0).astype(BF)
            sn[rows, H:] = v[:, H:].astype(BF)
            nx.append(go(remote(sn.at[rows, LO], n3, rn_s.at[2], rn_r.at[2], at_z(2))))
            nx.append(go(remote(sn.at[rows, HI], n4, rn_s.at[3], rn_r.at[3], at_z(-2))))
            continue
        sn[rows, :] = v.astype(BF)
        if q == 2:
            nx.append(go(remote(sn.at[rows, :], n1, rn_s.at[0], rn_r.at[0], at_z(1))))
        else:
            nx.append(go(remote(sn.at[rows, :], n2, rn_s.at[1], rn_r.at[1], at_z(-1))))

    ys1 = near_to_y(1, i4, ALLF, near1)
    for cp in nx:
        cp.wait_recv()
    own = tb[local_piece(0), :] + n1[...].astype(F32) + n2[...].astype(F32)
    lo = own[:, :H] + n3[...].astype(F32)
    hi = own[:, H:] + n4[...].astype(F32)
    for k in range(FAR):
        ff[k, :, :H] = lo[k * TOK:(k + 1) * TOK, :]
        ff[k, :, H:] = hi[k * TOK:(k + 1) * TOK, :]
    for k in range(FAR):
        fs[k] = ff[k].astype(BF)

    def dest(d):
        return (d + 2) % FAR

    x4l = go(remote(fs.at[dest(4), :, LO], c4l, rf_s.at[0], rf_r.at[0], at_z(2 * NEAR)))
    x4h = go(remote(fs.at[dest(4), :, HI], c4h, rf_s.at[1], rf_r.at[1], at_z(-2 * NEAR)))
    x3p = go(remote(fs.at[dest(3)], c3p, rf_s.at[2], rf_r.at[2], at_z(NEAR)))
    x3m = go(remote(fs.at[dest(-3)], c3m, rf_s.at[3], rf_r.at[3], at_z(-NEAR)))
    x1p = go(remote(fs.at[dest(1)], c1p, rf_s.at[4], rf_r.at[4], at_z(NEAR)))
    x1m = go(remote(fs.at[dest(-1)], c1m, rf_s.at[5], rf_r.at[5], at_z(-NEAR)))
    fw1 = y_forward(1, i4, ALLF, ys1)
    x3p.wait_recv()
    x4l.wait_recv()
    v = ff[dest(2)] + c3p[...].astype(F32)
    e2p[:, :H] = (v[:, :H] + c4l[...].astype(F32)).astype(BF)
    e2p[:, H:] = v[:, H:].astype(BF)
    x2p = go(remote(e2p, c2p, rf_s.at[6], rf_r.at[6], at_z(2 * NEAR)))
    x3m.wait_recv()
    x4h.wait_recv()
    v = ff[dest(-2)] + c3m[...].astype(F32)
    e2m[:, :H] = v[:, :H].astype(BF)
    e2m[:, H:] = (v[:, H:] + c4h[...].astype(F32)).astype(BF)
    x2m = go(remote(e2m, c2m, rf_s.at[7], rf_r.at[7], at_z(-2 * NEAR)))
    for cp in fw1:
        cp.wait_recv()
    for b in range(NY):
        merge(i4, IN, b, 0)
        merge(i4, IN, b, 1)
    dwg[...] = lax.dot_general(gg[...], IN[...], TN, preferred_element_type=F32).astype(BF)
    dwu[...] = lax.dot_general(gu[...], IN[...], TN, preferred_element_type=F32).astype(BF)
    total = ff[2]
    for cp, ref in ((x1p, c1p), (x1m, c1m), (x2p, c2p), (x2m, c2m)):
        cp.wait_recv()
        total = total + ref[...].astype(F32)
    gi[...] = total.astype(BF)

    for cp in pending:
        cp.wait_send()


def store(*refs):
    for src, dst in zip(refs[:4], refs[4:]):
        dst[...] = src[...]


def local(inputs, grad_out, gate, up, gate_weight, up_weight, down_weight):
    anyspec = pl.BlockSpec(memory_space=pl.ANY)
    V = pltpu.VMEM
    dma = pltpu.SemaphoreType.DMA
    four = V((TOK, D), BF)
    scratch = [
        V((NY, NEAR, FAR, TOK, D), BF), V((NY, NEAR, FAR, TOK, D), BF),
        V((TOKENS, D), BF), V((TOKENS, D), BF),
        V((F, D), BF), V((F, D), BF), V((F, D), BF),
        V((TOKENS, F), BF), V((TOKENS, F), BF),
        V((TOKENS, F), F32), V((TOKENS, F), F32), V((TOKENS, F), BF),
        V((ROWS, EB, F), BF), V((ROWS, 2 * EB, F), BF), V((ROWS, EB, F), BF),
        V((ROWS, EB, F), BF), V((ROWS, 2 * EB, F), BF), V((ROWS, EB, F), BF),
        V((ROWS, EB, F), BF), V((ROWS, 2 * EB, F), BF), V((ROWS, EB, F), BF),
        V((TOKENS, F), BF), V((TOKENS, F), BF),
        V((YB, D), BF), V((YB, D), BF), V((YB, D), BF),
        V((YB, D), BF), V((YB, D), BF), V((YB, D), BF),
        V((YB, D), F32), V((YB, D), BF),
        V((PB, D), BF), V((PB, D), BF), V((PB, H), BF), V((PB, H), BF),
        V((FAR, TOK, D), BF), V((FAR, TOK, D), F32),
        four, four, four, four, four, four, V((TOK, H), BF), V((TOK, H), BF), four, four,
        dma((7,)),
        dma((2, 4)), dma((2, 4)), dma((2, 2, 2)), dma((2, 2, 2)), dma((4, 4)), dma((4, 4)), dma((2, 4)), dma((2, 4)),
        dma((2, 4, 2)), dma((2, 4, 2)), dma((2, 4, 2)), dma((2, 4, 2)),
        dma((2, ROWS)), dma((2, ROWS)), dma((3, ROWS)), dma((3, ROWS)), dma((3, ROWS)), dma((3, ROWS)),
        dma((6,)), dma((6,)), dma((4,)), dma((4,)), dma((8,)), dma((8,)),
    ]
    shapes = (
        jax.ShapeDtypeStruct((TOK, D), BF),
        jax.ShapeDtypeStruct((F, D), BF),
        jax.ShapeDtypeStruct((F, D), BF),
        jax.ShapeDtypeStruct((F, D), BF),
    )
    vm = pl.BlockSpec(memory_space=pltpu.VMEM)
    args = (inputs, grad_out, gate, up, gate_weight.T, up_weight.T, down_weight)
    made = pl.pallas_call(
        kernel,
        out_shape=shapes,
        in_specs=[anyspec] * 7,
        out_specs=[vm] * 4,
        scratch_shapes=scratch,
        compiler_params=pltpu.CompilerParams(
            collective_id=0, has_side_effects=True, vmem_limit_bytes=40 * 1024 * 1024
        ),
    )(*[pltpu.with_memory_space_constraint(x, pltpu.HBM) for x in args])
    gi, dwg, dwu, dwd = pl.pallas_call(
        store,
        out_shape=shapes,
        in_specs=[vm] * 4,
        out_specs=[vm] * 4,
    )(*[pltpu.with_memory_space_constraint(x, pltpu.VMEM) for x in made])
    return gi, dwg.T, dwu.T, dwd


def solution(mesh):
    return jax.shard_map(
        local,
        mesh=mesh,
        in_specs=(
            P("col", "row"), P("col", "row"), P("row", "col"), P("row", "col"),
            P("row", "col"), P("row", "col"), P("col", "row"),
        ),
        out_specs=(P("col", "row"), P("row", "col"), P("row", "col"), P("col", "row")),
        check_vma=False,
    )
```

```python
import jax
import jax.numpy as jnp
from jax import lax
from jax.experimental import pallas as pl
from jax.experimental.pallas import tpu as pltpu
from jax.sharding import PartitionSpec as P

MESH = pl.DeviceIdType.MESH
BF = jnp.bfloat16
F32 = jnp.float32

ROWS = 8
NY, NZ = 4, 32
NEAR, FAR = 4, 8
TOK = 4
TOKENS = 512
D = 1024
F = 240
H = D // 2
YB = 128
PB = 32
RB = 64
EB = YB // 8


NT = (((1,), (1,)), ((), ()))
TN = (((0,), (0,)), ((), ()))


def al(x, n):
    return pl.multiple_of(x, n)


def kernel(
    in_hbm, out_hbm, gate_hbm, up_hbm, wg_hbm, wu_hbm, wd_hbm,
    gi, dwg, dwu, dwd,
    o4, i4, OUT, IN, wg, wu, wd, gate, up, fa, fb, hid,
    hp0, hpa, hpb, hr0, hra, hrb, gh0, gha, ghb, gg, gu, s2, sp, sm, r2, rm, rp, tp, tm, tb, sn, n1, n2, n3, n4,
    fs, ff, c1p, c1m, c2p, c2m, c3p, c3m, c4l, c4h, e2p, e2m,
    ld_sem,
    far_s, far_r, fw_s, fw_r, q_s, q_r, near_s, near_r, y_s, y_r, f_s, f_r,
    gu_s, gu_r, hp_s, hp_r, gh_s, gh_r,
    ry_s, ry_r, rn_s, rn_r, rf_s, rf_r,
):
    r = lax.axis_index("row")
    c = lax.axis_index("col")
    y = c // NZ
    z = c % NZ

    def at_z(dz):
        return (r, y * NZ + (z + dz + NZ) % NZ)

    def at_y(dy, dz=0):
        return (r, ((y + dy + NY) % NY) * NZ + (z + dz + NZ) % NZ)

    def at_row(dr):
        return ((r + dr) % ROWS, c)

    def remote(src, dst, ss, rs, dev):
        return pltpu.make_async_remote_copy(
            src_ref=src, dst_ref=dst, send_sem=ss, recv_sem=rs, device_id=dev, device_id_type=MESH
        )

    barrier = pltpu.get_barrier_semaphore()
    partners = [at_z(d) for d in (8, -8, 4, -4, 2, -2, 1, -1)] + [at_y(d) for d in (2, 1, -1)]
    partners += [at_y(dy, dz) for dy in (2, 1, -1) for dz in (2, -2, 1, -1)]
    partners += [at_row(k) for k in range(1, ROWS)]
    for dev in partners:
        pl.semaphore_signal(barrier, inc=1, device_id=dev, device_id_type=MESH)

    loads = [
        pltpu.make_async_copy(out_hbm, o4.at[0, 0, 2], ld_sem.at[0]),
        pltpu.make_async_copy(gate_hbm, gate.at[pl.ds(al(r * RB, RB), RB), :], ld_sem.at[1]),
        pltpu.make_async_copy(up_hbm, up.at[pl.ds(al(r * RB, RB), RB), :], ld_sem.at[2]),
        pltpu.make_async_copy(in_hbm, i4.at[0, 0, 2], ld_sem.at[3]),
        pltpu.make_async_copy(wd_hbm, wd, ld_sem.at[4]),
        pltpu.make_async_copy(wg_hbm, wg, ld_sem.at[5]),
        pltpu.make_async_copy(wu_hbm, wu, ld_sem.at[6]),
    ]
    for cp in loads:
        cp.start()
    loads[0].wait()
    pl.semaphore_wait(barrier, len(partners))

    pending = []

    def go(cp):
        cp.start()
        pending.append(cp)
        return cp

    LO, HI = pl.ds(0, H), pl.ds(H, H)

    DY = (0, -1, 1, 2)
    FIRST, LAST, SHIFTED, ALLF = pl.ds(0, 5), pl.ds(5, 3), pl.ds(4, 3), pl.ds(0, FAR)

    def far_direct(a, buf):
        return [
            go(remote(buf.at[0, 0, 2], buf.at[0, 0, slot], far_s.at[a, j], far_r.at[a, j], at_z(NEAR * d)))
            for j, (d, slot) in enumerate(((2, 0), (-2, 4), (1, 1), (-1, 3)))
        ]

    def far_forward(a, buf, direct):
        out = []
        for j, (d, src, dst, cols) in enumerate(((1, 0, 7, LO), (-1, 4, 5, HI))):
            direct[j].wait_recv()
            out.append(
                go(remote(buf.at[0, 0, src], buf.at[0, 0, dst], fw_s.at[a, j, 0], fw_r.at[a, j, 0], at_z(NEAR * d)))
            )
            out.append(
                go(
                    remote(
                        buf.at[0, 0, src, :, cols], buf.at[0, 0, 6, :, cols],
                        fw_s.at[a, j, 1], fw_r.at[a, j, 1], at_z(2 * NEAR * d),
                    )
                )
            )
        return out

    def near_send(a, buf, part):
        return [
            go(remote(buf.at[0, 0, part], buf.at[0, p, part], near_s.at[a, p], near_r.at[a, p], at_z(dz)))
            for p, dz in ((1, 1), (2, -1), (3, 2))
        ]

    def y_send(a, buf, part, p):
        return [
            go(remote(buf.at[0, p, part], buf.at[b, p, part], y_s.at[a, p, j], y_r.at[a, p, j], at_y(dy)))
            for j, (b, dy) in enumerate(((1, 1), (2, -1)))
        ]

    def y_forward(a, buf, part, ys):
        out = []
        for p in range(NEAR):
            for j, (b, dy, cols) in enumerate(((1, 1, LO), (2, -1, HI))):
                ys[p][j].wait_recv()
                out.append(
                    go(
                        remote(
                            buf.at[b, p, part, :, cols], buf.at[3, p, part, :, cols],
                            f_s.at[a, p, j], f_r.at[a, p, j], at_y(dy),
                        )
                    )
                )
        return out

    def near_to_y(a, buf, part, near):
        ys = [y_send(a, buf, part, 0)]
        for p in (1, 2, 3):
            near[p - 1].wait_recv()
            ys.append(y_send(a, buf, part, p))
        return ys

    def merge(buf, full, b, half):
        for p in range(NEAR):
            block = jnp.concatenate([buf[b, p, 4 * half + j].astype(F32) for j in range(4)], axis=0)
            at = b * YB + p * PB + half * 4 * TOK
            full[at:at + 4 * TOK, :] = block.astype(BF)

    far0 = far_direct(0, o4)

    loads[1].wait()
    loads[2].wait()
    mine = pl.ds(al(r * RB, RB), RB)
    gus = []
    for a, ref in enumerate((gate, up)):
        for k in range(1, ROWS):
            gus.append(go(remote(ref.at[mine, :], ref.at[mine, :], gu_s.at[a, k], gu_r.at[a, k], at_row(k))))

    ffw0 = far_forward(0, o4, far0)
    far0[2].wait_recv()
    far0[3].wait_recv()
    near0 = near_send(0, o4, FIRST)
    ys0 = near_to_y(0, o4, FIRST, near0)
    merge(o4, OUT, 0, 0)
    for cp in ffw0:
        cp.wait_recv()
    rest = [[None] * NEAR for _ in range(NY)]
    for b, dy in ((3, 2), (1, 1), (2, -1), (0, 0)):
        for p, dz, part in ((3, -2, SHIFTED), (1, 1, LAST), (2, -1, LAST), (0, 0, LAST)):
            if b or p:
                rest[b][p] = go(
                    remote(o4.at[0, 0, part], o4.at[b, p, LAST], q_s.at[b, p], q_r.at[b, p], at_y(dy, dz))
                )
    fw0 = y_forward(0, o4, FIRST, ys0)
    merge(o4, OUT, 1, 0)
    merge(o4, OUT, 2, 0)

    for cp in gus:
        cp.wait_recv()
    ri = lax.broadcasted_iota(jnp.int32, (YB, YB), 0)
    ci = lax.broadcasted_iota(jnp.int32, (YB, YB), 1)
    near_i = ri // PB
    step = jnp.where(near_i == 0, 0, jnp.where(near_i == 1, -1, jnp.where(near_i == 2, 1, -2)))
    want = ((z + step + NEAR * ((ri // TOK) % FAR - 2) + 2 * NZ) % NZ) * TOK + ri % TOK
    perm = jnp.where(ci == want, 1.0, 0.0).astype(BF)
    for b in range(NY):
        src = pl.ds(al(((y + DY[b] + NY) % NY) * YB, YB), YB)
        rows = pl.ds(b * YB, YB)
        g = jnp.dot(perm, gate[src, :], preferred_element_type=F32)
        u = jnp.dot(perm, up[src, :], preferred_element_type=F32)
        s = 1.0 / (1.0 + jnp.exp(-g))
        act = g * s
        fa[rows, :] = u * s * (1.0 + g * (1.0 - s))
        fb[rows, :] = act
        hid[rows, :] = (act * u).astype(BF)

    loads[4].wait()

    def y_rows(b):
        return pl.ds(b * YB, YB)

    def arrived(b):
        for cp in rest[b]:
            if cp is not None:
                cp.wait_recv()
        merge(o4, OUT, b, 1)

    def hidden_block(b, dst, i):
        part = lax.dot_general(OUT[y_rows(b), :], wd[...], NT, preferred_element_type=F32)
        dst[:, i * EB:(i + 1) * EB, :] = part.astype(BF).reshape(ROWS, EB, F)

    def row_out(src, dst, b):
        cps = []
        for k in range(1, ROWS):
            cps.append(go(remote(src.at[(r + k) % ROWS], dst.at[k], hp_s.at[b, k], hp_r.at[b, k], at_row(k))))
        return cps

    def row_back(cps, own, got, dst, b):
        acc = own[r].astype(F32)
        for k in range(1, ROWS):
            cps[k - 1].wait_recv()
            acc = acc + got[k].astype(F32)
        dst[r] = acc.astype(BF)
        return [go(remote(dst.at[r], dst.at[r], gh_s.at[b, k], gh_r.at[b, k], at_row(k))) for k in range(1, ROWS)]

    def gated(b, src, i):
        rows = y_rows(b)
        v = src[:, i * EB:(i + 1) * EB, :].reshape(YB, F).astype(F32)
        gg[rows, :] = (v * fa[rows, :]).astype(BF)
        gu[rows, :] = (v * fb[rows, :]).astype(BF)

    def partial(b):
        rows = y_rows(b)
        return jnp.dot(gg[rows, :], wg[...], preferred_element_type=F32) + jnp.dot(
            gu[rows, :], wu[...], preferred_element_type=F32
        )

    arrived(0)
    hidden_block(0, hp0, 0)
    x0 = row_out(hp0, hr0, 0)
    arrived(1)
    hidden_block(1, hpa, 0)
    arrived(2)
    hidden_block(2, hpa, 1)
    xa = row_out(hpa, hra, 1)
    loads[3].wait()
    far1 = far_direct(1, i4)
    for cp in fw0:
        cp.wait_recv()
    merge(o4, OUT, 3, 0)
    arrived(3)
    hidden_block(3, hpb, 0)
    xb = row_out(hpb, hrb, 2)
    g0 = row_back(x0, hp0, hr0, gh0, 0)
    ga = row_back(xa, hpa, hra, gha, 1)
    gb = row_back(xb, hpb, hrb, ghb, 2)
    ffw1 = far_forward(1, i4, far1)

    loads[5].wait()
    loads[6].wait()
    for cp in ga:
        cp.wait_recv()
    gated(2, gha, 1)
    tp[...] = partial(2)
    sp[:, H:] = tp[:, H:].astype(BF)
    go_p = go(remote(sp.at[:, HI], rm.at[:, HI], ry_s.at[0], ry_r.at[0], at_y(1)))
    gated(1, gha, 0)
    tm[...] = partial(1)
    sm[:, :H] = tm[:, :H].astype(BF)
    go_m = go(remote(sm.at[:, LO], rp.at[:, LO], ry_s.at[1], ry_r.at[1], at_y(-1)))
    for cp in g0:
        cp.wait_recv()
    gated(0, gh0, 0)
    tb[...] = partial(0)
    for cp in gb:
        cp.wait_recv()
    gated(3, ghb, 0)

    def local_piece(p):
        return pl.ds(p * PB, PB)

    RQ = (3, 2, 1, 0)
    s2[...] = partial(3).astype(BF)
    half_y = []
    for i, q in enumerate(RQ):
        rows = local_piece(q)
        half_y.append(
            [
                go(remote(s2.at[rows, cols], r2.at[rows, cols], ry_s.at[2 + 2 * i + j], ry_r.at[2 + 2 * i + j], at_y(dy)))
                for j, (cols, dy) in enumerate(((LO, 1), (HI, -1)))
            ]
        )
    far_y = []
    for i, q in enumerate(RQ):
        rows = local_piece(q)
        half_y[i][0].wait_recv()
        sp[rows, :H] = (tp[rows, :H] + r2[rows, :H].astype(F32)).astype(BF)
        one = go(remote(sp.at[rows, LO], rm.at[rows, LO], ry_s.at[10 + 2 * i], ry_r.at[10 + 2 * i], at_y(1)))
        half_y[i][1].wait_recv()
        sm[rows, H:] = (tm[rows, H:] + r2[rows, H:].astype(F32)).astype(BF)
        two = go(remote(sm.at[rows, HI], rp.at[rows, HI], ry_s.at[11 + 2 * i], ry_r.at[11 + 2 * i], at_y(-1)))
        far_y.append((one, two))
    for cp in far1[2:] + ffw1:
        cp.wait_recv()
    near1 = near_send(1, i4, ALLF)
    dwd[...] = lax.dot_general(hid[...], OUT[...], TN, preferred_element_type=F32).astype(BF)

    go_p.wait_recv()
    go_m.wait_recv()
    nx = []
    for i, q in enumerate(RQ):
        rows = local_piece(q)
        far_y[i][0].wait_recv()
        far_y[i][1].wait_recv()
        v = tb[rows, :] + rm[rows, :].astype(F32) + rp[rows, :].astype(F32)
        if q == 0:
            tb[rows, :] = v
            continue
        if q == 3:
            sn[rows, :H] = jnp.concatenate([v[TOK:, :H], v[:TOK, :H]], axis=0).astype(BF)
            sn[rows, H:] = v[:, H:].astype(BF)
            nx.append(go(remote(sn.at[rows, LO], n3, rn_s.at[2], rn_r.at[2], at_z(2))))
            nx.append(go(remote(sn.at[rows, HI], n4, rn_s.at[3], rn_r.at[3], at_z(-2))))
            continue
        sn[rows, :] = v.astype(BF)
        if q == 2:
            nx.append(go(remote(sn.at[rows, :], n1, rn_s.at[0], rn_r.at[0], at_z(1))))
        else:
            nx.append(go(remote(sn.at[rows, :], n2, rn_s.at[1], rn_r.at[1], at_z(-1))))

    ys1 = near_to_y(1, i4, ALLF, near1)
    for cp in nx:
        cp.wait_recv()
    own = tb[local_piece(0), :] + n1[...].astype(F32) + n2[...].astype(F32)
    lo = own[:, :H] + n3[...].astype(F32)
    hi = own[:, H:] + n4[...].astype(F32)
    for k in range(FAR):
        ff[k, :, :H] = lo[k * TOK:(k + 1) * TOK, :]
        ff[k, :, H:] = hi[k * TOK:(k + 1) * TOK, :]
    for k in range(FAR):
        fs[k] = ff[k].astype(BF)

    def dest(d):
        return (d + 2) % FAR

    x4l = go(remote(fs.at[dest(4), :, LO], c4l, rf_s.at[0], rf_r.at[0], at_z(2 * NEAR)))
    x4h = go(remote(fs.at[dest(4), :, HI], c4h, rf_s.at[1], rf_r.at[1], at_z(-2 * NEAR)))
    x3p = go(remote(fs.at[dest(3)], c3p, rf_s.at[2], rf_r.at[2], at_z(NEAR)))
    x3m = go(remote(fs.at[dest(-3)], c3m, rf_s.at[3], rf_r.at[3], at_z(-NEAR)))
    x1p = go(remote(fs.at[dest(1)], c1p, rf_s.at[4], rf_r.at[4], at_z(NEAR)))
    x1m = go(remote(fs.at[dest(-1)], c1m, rf_s.at[5], rf_r.at[5], at_z(-NEAR)))
    fw1 = y_forward(1, i4, ALLF, ys1)
    x3p.wait_recv()
    x4l.wait_recv()
    v = ff[dest(2)] + c3p[...].astype(F32)
    e2p[:, :H] = (v[:, :H] + c4l[...].astype(F32)).astype(BF)
    e2p[:, H:] = v[:, H:].astype(BF)
    x2p = go(remote(e2p, c2p, rf_s.at[6], rf_r.at[6], at_z(2 * NEAR)))
    x3m.wait_recv()
    x4h.wait_recv()
    v = ff[dest(-2)] + c3m[...].astype(F32)
    e2m[:, :H] = v[:, :H].astype(BF)
    e2m[:, H:] = (v[:, H:] + c4h[...].astype(F32)).astype(BF)
    x2m = go(remote(e2m, c2m, rf_s.at[7], rf_r.at[7], at_z(-2 * NEAR)))
    for cp in fw1:
        cp.wait_recv()
    for b in range(NY):
        merge(i4, IN, b, 0)
        merge(i4, IN, b, 1)
    dwg[...] = lax.dot_general(gg[...], IN[...], TN, preferred_element_type=F32).astype(BF)
    dwu[...] = lax.dot_general(gu[...], IN[...], TN, preferred_element_type=F32).astype(BF)
    total = ff[2]
    for cp, ref in ((x1p, c1p), (x1m, c1m), (x2p, c2p), (x2m, c2m)):
        cp.wait_recv()
        total = total + ref[...].astype(F32)
    gi[...] = total.astype(BF)

    for cp in pending:
        cp.wait_send()


def store(*refs):
    for src, dst in zip(refs[:4], refs[4:]):
        dst[...] = src[...]


def local(inputs, grad_out, gate, up, gate_weight, up_weight, down_weight):
    anyspec = pl.BlockSpec(memory_space=pl.ANY)
    V = pltpu.VMEM
    dma = pltpu.SemaphoreType.DMA
    four = V((TOK, D), BF)
    scratch = [
        V((NY, NEAR, FAR, TOK, D), BF), V((NY, NEAR, FAR, TOK, D), BF),
        V((TOKENS, D), BF), V((TOKENS, D), BF),
        V((F, D), BF), V((F, D), BF), V((F, D), BF),
        V((TOKENS, F), BF), V((TOKENS, F), BF),
        V((TOKENS, F), F32), V((TOKENS, F), F32), V((TOKENS, F), BF),
        V((ROWS, EB, F), BF), V((ROWS, 2 * EB, F), BF), V((ROWS, EB, F), BF),
        V((ROWS, EB, F), BF), V((ROWS, 2 * EB, F), BF), V((ROWS, EB, F), BF),
        V((ROWS, EB, F), BF), V((ROWS, 2 * EB, F), BF), V((ROWS, EB, F), BF),
        V((TOKENS, F), BF), V((TOKENS, F), BF),
        V((YB, D), BF), V((YB, D), BF), V((YB, D), BF),
        V((YB, D), BF), V((YB, D), BF), V((YB, D), BF),
        V((YB, D), F32), V((YB, D), F32), V((YB, D), F32), V((YB, D), BF),
        V((PB, D), BF), V((PB, D), BF), V((PB, H), BF), V((PB, H), BF),
        V((FAR, TOK, D), BF), V((FAR, TOK, D), F32),
        four, four, four, four, four, four, V((TOK, H), BF), V((TOK, H), BF), four, four,
        dma((7,)),
        dma((2, 4)), dma((2, 4)), dma((2, 2, 2)), dma((2, 2, 2)), dma((4, 4)), dma((4, 4)), dma((2, 4)), dma((2, 4)),
        dma((2, 4, 2)), dma((2, 4, 2)), dma((2, 4, 2)), dma((2, 4, 2)),
        dma((2, ROWS)), dma((2, ROWS)), dma((3, ROWS)), dma((3, ROWS)), dma((3, ROWS)), dma((3, ROWS)),
        dma((18,)), dma((18,)), dma((4,)), dma((4,)), dma((8,)), dma((8,)),
    ]
    shapes = (
        jax.ShapeDtypeStruct((TOK, D), BF),
        jax.ShapeDtypeStruct((F, D), BF),
        jax.ShapeDtypeStruct((F, D), BF),
        jax.ShapeDtypeStruct((F, D), BF),
    )
    vm = pl.BlockSpec(memory_space=pltpu.VMEM)
    args = (inputs, grad_out, gate, up, gate_weight.T, up_weight.T, down_weight)
    made = pl.pallas_call(
        kernel,
        out_shape=shapes,
        in_specs=[anyspec] * 7,
        out_specs=[vm] * 4,
        scratch_shapes=scratch,
        compiler_params=pltpu.CompilerParams(
            collective_id=0, has_side_effects=True, vmem_limit_bytes=40 * 1024 * 1024
        ),
    )(*[pltpu.with_memory_space_constraint(x, pltpu.HBM) for x in args])
    gi, dwg, dwu, dwd = pl.pallas_call(
        store,
        out_shape=shapes,
        in_specs=[vm] * 4,
        out_specs=[vm] * 4,
    )(*[pltpu.with_memory_space_constraint(x, pltpu.VMEM) for x in made])
    return gi, dwg.T, dwu.T, dwd


def solution(mesh):
    return jax.shard_map(
        local,
        mesh=mesh,
        in_specs=(
            P("col", "row"), P("col", "row"), P("row", "col"), P("row", "col"),
            P("row", "col"), P("row", "col"), P("col", "row"),
        ),
        out_specs=(P("col", "row"), P("row", "col"), P("row", "col"), P("col", "row")),
        check_vma=False,
    )
```
